32 devices in a mesh: span: 8 (over z, x), wall: 4 (over y, core).
Axes of the slice: x: 2, y: 2, z: 4, core: 2. Of those that a mesh axis runs over, the one named last changes fastest.
Arguments:
- velocity: float32 [3, 2, 128, 2048], P(None, None, 'wall', 'span'), may hold values from -6 to 6
- metric: float32 [128], P('wall'), may hold values from 0.5 to 2
Outputs:
- conv: float32 [3, 2, 128, 2048], P(None, None, 'wall', 'span')
- flux: float32 [3, 2, 128, 2048], P(None, None, 'wall', 'span')
The draws below stay inside these ranges and needn't reach their ends.
All inputs are finite; a program needn't handle non-finite values.
Results may differ from the reference program's by a relative error of at most 0.00014.
Values sent between devices are 32-bit elements; how exact they have to be, the bound alone decides.
A program may use at most 64 MiB of HBM per device.

```python
import math
import jax
import jax.numpy as jnp
from jax import lax

XS = 2
NY = 128
NZ = 2048


def levels(stream_key, dims, shards, low, top_value):
    loudness = 1.0
    for axis_at, blocks in shards:
        draws = jax.random.uniform(jax.random.fold_in(jax.random.fold_in(stream_key, 6), axis_at), (blocks,), jnp.float32, low / len(shards), top_value / len(shards))
        loudness = loudness * jnp.repeat(jnp.exp(draws), dims[axis_at] // blocks).reshape((-1,) + (1,) * (len(dims) - 1 - axis_at))
    return loudness


def normal_values(key, shape, deviation, reach, shards=(), kind=jnp.bfloat16):
    drawn = deviation * jax.random.normal(key, shape, jnp.float32)
    if shards:
        drawn = drawn * levels(key, shape, shards, -0.22, 0.18)
    return jnp.clip(drawn, -reach, reach).astype(kind)


def setup_inputs(seed: int = 0) -> dict:
    key_list = jax.random.split(jax.random.key(seed), 3)
    velocity = normal_values(key_list[0], (3, XS, NY, NZ), 1.0, 6.0, ((2, 4), (3, 8)), jnp.float32)
    metric = jnp.clip(jnp.exp(math.log(2.0) - 1.3862944 * jax.random.uniform(key_list[1], (NY,), jnp.float32) ** levels(key_list[1], (NY,), ((0, 4),), -0.2, 0.2)), 0.5, 2.0)
    return dict(velocity=velocity, metric=metric)


def plane_terms(velplane, metric):
    comp_u = velplane[0]
    comp_v = velplane[1]
    comp_w = velplane[2]
    prods = jnp.stack([comp_u * comp_u, comp_u * comp_v, comp_u * comp_w,
                       comp_v * comp_v, comp_v * comp_w, comp_w * comp_w])
    spec = jnp.fft.fft(prods, axis=-1)
    real_part = jnp.real(spec)
    imag_part = jnp.imag(spec)
    counter = jnp.arange(NZ, dtype=jnp.int32)
    signed = jnp.where(counter < NZ // 2, counter, counter - NZ)
    keep = (3 * jnp.abs(signed) < NZ).astype(jnp.float32)
    kappa = (2.0 * math.pi / NZ) * signed.astype(jnp.float32)
    real_part = real_part * keep
    imag_part = imag_part * keep

    def deriv_y(field):
        padded = jnp.pad(field, ((1, 1), (0, 0)))
        return (padded[2:] - padded[:-2]) * metric[:, None]

    conv_real = [deriv_y(real_part[1]) - kappa * imag_part[2],
                 deriv_y(real_part[3]) - kappa * imag_part[4],
                 deriv_y(real_part[4]) - kappa * imag_part[5]]
    conv_imag = [deriv_y(imag_part[1]) + kappa * real_part[2],
                 deriv_y(imag_part[3]) + kappa * real_part[4],
                 deriv_y(imag_part[4]) + kappa * real_part[5]]
    all_real = jnp.stack(conv_real + [real_part[0], real_part[1], real_part[2]])
    all_imag = jnp.stack(conv_imag + [imag_part[0], imag_part[1], imag_part[2]])
    back = jnp.fft.ifft(lax.complex(all_real, all_imag), axis=-1)
    return jnp.real(back)


def reference(velocity, metric):
    planes_first = jnp.moveaxis(velocity, 1, 0)
    result = lax.map(lambda velplane: plane_terms(velplane, metric), planes_first)
    result = jnp.moveaxis(result, 0, 1).astype(jnp.float32)
    return (result[:3], result[3:])
```

```python
import functools
import math

import jax
import jax.numpy as jnp
import numpy as np
from jax import lax
from jax.experimental import pallas as pl
from jax.experimental.pallas import tpu as pltpu
from jax.sharding import PartitionSpec as P

MESH = pl.DeviceIdType.MESH


def split_bf16(table):
    high = table.astype(jnp.bfloat16)
    low = (table - np.asarray(high, np.float64)).astype(jnp.bfloat16)
    return high, low


def make_tables(count, local_len):
    total = count * local_len
    halves = count // 2 + 1
    k1 = np.arange(halves, dtype=np.int64)[:, None]
    m = np.arange(local_len, dtype=np.int64)[None, :]
    angle = 2.0 * math.pi / total * (k1 * m % total)
    wave = k1 + count * m
    signed = np.where(wave < total // 2, wave, wave - total)
    weight = np.where((k1 == 0) | (2 * k1 == count), 1.0, 2.0) / total
    keep = (3 * np.abs(signed) < total) * weight
    kappa = 2.0 * math.pi / total * signed * keep
    small = np.stack([np.cos(angle), -np.sin(angle), keep, kappa]).astype(np.float32)
    small = np.pad(small, ((0, 0), (0, -halves % 8), (0, 0)))
    phase = 2.0 * math.pi / local_len * (m.T * m % local_len)
    table = np.concatenate([np.cos(phase), -np.sin(phase)], axis=1)
    return small, np.stack(split_bf16(table))


def weighted(coeffs, values):
    acc = None
    for coeff, value in zip(coeffs, values):
        if abs(coeff) < 1e-12:
            continue
        if abs(abs(coeff) - 1.0) < 1e-12:
            if acc is None:
                acc = value if coeff > 0 else -value
            else:
                acc = acc + value if coeff > 0 else acc - value
        else:
            term = value * np.float32(coeff)
            acc = term if acc is None else acc + term
    return acc


def real_dft(values):
    n = len(values)
    if n == 1:
        return [(values[0], None)]
    half = n // 2
    sums = [values[p] + values[p + half] for p in range(half)]
    diffs = [values[p] - values[p + half] for p in range(half)]
    bins = [None] * (half + 1)
    for index, item in enumerate(real_dft(sums)):
        bins[2 * index] = item
    for k in range(1, half + 1, 2):
        cosines = [math.cos(2 * math.pi * p * k / n) for p in range(half)]
        sines = [-math.sin(2 * math.pi * p * k / n) for p in range(half)]
        bins[k] = (weighted(cosines, diffs), weighted(sines, diffs))
    return bins


def real_inverse(bins, n):
    if n == 1:
        return [bins[0][0]]
    if n == 2:
        return [bins[0][0] + bins[1][0], bins[0][0] - bins[1][0]]
    half = n // 2
    even = real_inverse(bins[0::2], half)
    odd = []
    ks = list(range(1, half, 2))
    for p in range(half):
        coeffs = [math.cos(2 * math.pi * p * k / n) for k in ks]
        coeffs += [-math.sin(2 * math.pi * p * k / n) for k in ks]
        odd.append(weighted(coeffs, [bins[k][0] for k in ks] + [bins[k][1] for k in ks]))
    return [even[p] + odd[p] for p in range(half)] + [even[p] - odd[p] for p in range(half)]


def dft_rows(rows, dft):
    high = rows.astype(jnp.bfloat16)
    low = (rows - high.astype(jnp.float32)).astype(jnp.bfloat16)
    dot = functools.partial(jnp.dot, preferred_element_type=jnp.float32)
    return dot(high, dft[0]) + dot(low, dft[0]) + dot(high, dft[1])


def kernel(
    dims, source, velocity_hbm, metric_hbm, small_hbm, dft_hbm, flux, conv,
    metric, small, planes, ends, wedge, recv, recv_ends, halo, dft, wave_in, wave, obuf,
    local_sem, send_sem, recv_sem, esend_sem, erecv_sem, hsend_sem, hrecv_sem, mine_sem, osend_sem,
    orecv_sem,
):
    count, walls, xs_len, chunk, local_len = dims
    halves = count // 2 + 1
    per_xs = count // xs_len
    span = lax.axis_index("span")
    wall = lax.axis_index("wall")
    place = lax.rem(span, per_xs)
    has_below, has_above = wall > 0, wall < walls - 1

    def wall_at(step):
        return lax.rem(wall + walls + step, walls)

    order = sorted(range(1, count), key=lambda d: abs(d - count // 2))

    def block(ref, index):
        if chunk % 8:
            return ref.at[index]
        at = pl.multiple_of(lax.rem(index, per_xs) * chunk, chunk)
        return ref.at[:, index // per_xs, pl.ds(at, chunk), :]

    barrier = pltpu.get_barrier_semaphore()
    for d in order:
        pl.semaphore_signal(
            barrier, inc=1, device_id=(lax.rem(span + d, count), wall), device_id_type=MESH
        )

    for there, at, step in ((has_below, 0, -1), (has_above, per_xs - 1, 1)):

        @pl.when(there)
        def _():
            @pl.when(place == at)
            def _():
                for p in range(count):
                    pl.semaphore_signal(
                        barrier, inc=1, device_id=(p, wall_at(step)), device_id_type=MESH
                    )

    stage = pltpu.make_async_copy(velocity_hbm, planes, local_sem.at[4])
    stage.start()
    own = pltpu.make_async_copy(block(source, span), recv.at[span], local_sem.at[1])
    own.start()
    load = pltpu.make_async_copy(dft_hbm, dft, local_sem.at[0])
    load.start()
    tables = pltpu.make_async_copy(small_hbm, small, local_sem.at[2])
    tables.start()
    scales = pltpu.make_async_copy(metric_hbm, metric, local_sem.at[3])
    scales.start()

    stage.wait()
    none = jnp.zeros((1, local_len), jnp.float32)

    def plane(x, at):
        if at < 0 or at >= per_xs * chunk:
            return [none] * 3
        return [planes[comp, x, pl.ds(at, 1), :] for comp in range(3)]

    for x in range(xs_len):
        for j in range(per_xs):
            rows = plane(x, j * chunk - 1) + plane(x, (j + 1) * chunk) + [none] * 2
            ends[x * per_xs + j] = jnp.concatenate(rows, axis=0)
        rows = plane(x, per_xs * chunk - 1) + [none] * 5
        wedge[0, x] = jnp.concatenate(rows, axis=0)
        rows = [none] * 3 + plane(x, 0) + [none] * 2
        wedge[1, x] = jnp.concatenate(rows, axis=0)

    sides = (wall + walls - 1) // walls + (2 * walls - 2 - wall) // walls
    pl.semaphore_wait(barrier, count - 1 + xs_len * sides)

    sends = []
    arrivals = [[] for _ in range(3)]
    for comp in range(3):
        for d in order:
            peer = lax.rem(span + d, count)
            copy = pltpu.make_async_remote_copy(
                src_ref=block(source, peer).at[comp],
                dst_ref=recv.at[span, comp],
                send_sem=send_sem.at[comp, d],
                recv_sem=recv_sem.at[comp, d],
                device_id=(peer, wall),
                device_id_type=MESH,
            )
            copy.start()
            arrivals[comp].append(copy)
    for d in order:
        peer = lax.rem(span + d, count)
        copy = pltpu.make_async_remote_copy(
            src_ref=ends.at[peer],
            dst_ref=recv_ends.at[span],
            send_sem=esend_sem.at[d],
            recv_sem=erecv_sem.at[d],
            device_id=(peer, wall),
            device_id_type=MESH,
        )
        copy.start()
        sends.append(copy)
    own_ends = pltpu.make_async_copy(ends.at[span], recv_ends.at[span], local_sem.at[5])
    own_ends.start()

    def halo_copy(side, x):
        if side == 0:
            target = (x * per_xs, wall_at(1))
        else:
            target = (x * per_xs + per_xs - 1, wall_at(-1))
        return pltpu.make_async_remote_copy(
            src_ref=wedge.at[side, x],
            dst_ref=halo.at[side, span],
            send_sem=hsend_sem.at[side, x],
            recv_sem=hrecv_sem.at[side, span],
            device_id=target,
            device_id_type=MESH,
        )

    def halo_arrival(side, p):
        return pltpu.make_async_remote_copy(
            src_ref=wedge.at[side, 0],
            dst_ref=halo.at[side, p],
            send_sem=hsend_sem.at[side, 0],
            recv_sem=hrecv_sem.at[side, p],
            device_id=(p, wall_at(2 * side - 1)),
            device_id_type=MESH,
        )

    for side, there in ((0, has_above), (1, has_below)):

        @pl.when(there)
        def _():
            for x in range(xs_len):
                halo_copy(side, x).start()

    load.wait()
    own.wait()
    tables.wait()
    scales.wait()

    def wait_component(comp):
        for copy in arrivals[comp]:
            copy.wait_recv()

    def wait_edges():
        own_ends.wait()
        for copy in sends:
            copy.wait_recv()
        for side, there, at in ((0, has_below, 0), (1, has_above, per_xs - 1)):

            @pl.when(there)
            def _():
                @pl.when(place == at)
                def _():
                    row = lax.broadcasted_iota(jnp.int32, (8, local_len), 0)
                    taken = row < 3 if side == 0 else row >= 3
                    for p in range(count):
                        halo_arrival(side, p).wait_recv()
                        recv_ends[p] = jnp.where(taken, halo[side, p], recv_ends[p])

    row = lax.broadcasted_iota(jnp.int32, (chunk, local_len), 0)
    scale = jnp.zeros((chunk, local_len), jnp.float32)
    for j in range(chunk):
        scale = jnp.where(row == j, metric[place * chunk + j], scale)

    def velocity(p, comp):
        return recv[p, comp]

    def product(first, second):
        return [velocity(p, first) * velocity(p, second) for p in range(count)]

    def slope(first, second):
        fields = []
        for p in range(count):
            edge = recv_ends[p]
            below = edge[first : first + 1] * edge[second : second + 1]
            above = edge[3 + first : 4 + first] * edge[3 + second : 4 + second]
            inner = velocity(p, first) * velocity(p, second)
            upper = jnp.concatenate([inner[1:], above], axis=0)
            lower = jnp.concatenate([below, inner[:-1]], axis=0)
            fields.append((upper - lower) * scale)
        return fields

    def twiddle(k):
        return small[0, pl.ds(k, 1), :], small[1, pl.ds(k, 1), :]

    def rows_of(ref, start, stop):
        return ref[:, start:stop].reshape(2 * (stop - start) * ref.shape[2], local_len)

    def forward(start, fields):
        for number, values in enumerate(fields):
            for k, (real, imag) in enumerate(real_dft(values)):
                at = (start + number) * halves + k
                tw_cos, tw_sin = twiddle(k)
                if imag is None:
                    wave_in[0, at, 0:chunk, :] = real * tw_cos
                    wave_in[1, at, 0:chunk, :] = real * tw_sin
                else:
                    wave_in[0, at, 0:chunk, :] = real * tw_cos - imag * tw_sin
                    wave_in[1, at, 0:chunk, :] = real * tw_sin + imag * tw_cos
        first, last = start * halves, (start + len(fields)) * halves
        both = dft_rows(rows_of(wave_in, first, last), dft)
        both = both.reshape(2, last - first, wave.shape[2], 2 * local_len)
        by_cos, by_sin = both[..., :local_len], both[..., local_len:]
        wave[0, first:last] = by_cos[0] - by_sin[1]
        wave[1, first:last] = by_sin[0] + by_cos[1]

    copies = []

    def deliver(group, number, filtered):
        slot = 3 * group + number
        for k in range(halves):
            real, imag = filtered(number, k)
            wave_in[0, k] = real
            wave_in[1, k] = imag
        both = dft_rows(rows_of(wave_in, 0, halves), dft)
        both = both.reshape(2, halves, wave.shape[2], 2 * local_len)
        by_cos, by_sin = both[..., :local_len], both[..., local_len:]
        bins = []
        for k in range(halves):
            real = by_cos[0, k] + by_sin[1, k]
            imag = by_cos[1, k] - by_sin[0, k]
            tw_cos, tw_sin = twiddle(k)
            bins.append((real * tw_cos + imag * tw_sin, imag * tw_cos - real * tw_sin))
        for p, value in enumerate(real_inverse(bins, count)):
            obuf[slot, p] = value[0:chunk]
        target = block((flux, conv)[group], span).at[number]
        mine = pltpu.make_async_copy(obuf.at[slot, span], target, mine_sem.at[slot])
        mine.start()
        copies.append(mine)
        for d in order:
            peer = lax.rem(span + d, count)
            copy = pltpu.make_async_remote_copy(
                src_ref=obuf.at[slot, peer],
                dst_ref=target,
                send_sem=osend_sem.at[slot, d],
                recv_sem=orecv_sem.at[slot, d],
                device_id=(peer, wall),
                device_id_type=MESH,
            )
            copy.start()
            copies.append(copy)

    def keep_only(number, k):
        keep = small[2, pl.ds(k, 1), :]
        at = number * halves + k
        return wave[0, at] * keep, wave[1, at] * keep

    def divergence(number, k):
        keep, kappa = small[2, pl.ds(k, 1), :], small[3, pl.ds(k, 1), :]
        at_y = ((3, 4, 6)[number]) * halves + k
        at_z = ((2, 5, 7)[number]) * halves + k
        real = wave[0, at_y] * keep - wave[1, at_z] * kappa
        imag = wave[1, at_y] * keep + wave[0, at_z] * kappa
        return real, imag

    for comp in range(3):
        wait_component(comp)
        forward(comp, [product(0, comp)])
        deliver(0, comp, keep_only)
    wait_edges()
    forward(3, [slope(0, 1)])
    deliver(1, 0, divergence)
    forward(4, [slope(1, 1), product(1, 2)])
    deliver(1, 1, divergence)
    forward(6, [slope(1, 2), product(2, 2)])
    deliver(1, 2, divergence)

    for copy in sum(arrivals, sends):
        copy.wait_send()
    for side, there in ((0, has_above), (1, has_below)):

        @pl.when(there)
        def _():
            for x in range(xs_len):
                halo_copy(side, x).wait_send()

    for copy in copies:
        copy.wait()


def store(flux_in, conv_in, flux, conv, sem):
    copies = [
        pltpu.make_async_copy(flux_in, flux, sem.at[0]),
        pltpu.make_async_copy(conv_in, conv, sem.at[1]),
    ]
    for copy in copies:
        copy.start()
    for copy in copies:
        copy.wait()


def body(walls, velocity, metric):
    count = lax.axis_size("span")
    _, xs_len, yl_len, local_len = velocity.shape
    per_xs = count // xs_len
    chunk = yl_len // per_xs
    halves = count // 2 + 1
    rows = 8 * ((chunk + 7) // 8)
    small, dft = make_tables(count, local_len)

    blocks = (count, 3, chunk, local_len)
    out_shape = velocity.shape
    source = velocity
    if chunk % 8:
        source = velocity.reshape(3, xs_len, per_xs, chunk, local_len)
        source = source.transpose(1, 2, 0, 3, 4).reshape(blocks)
        out_shape = blocks

    anywhere = pl.BlockSpec(memory_space=pl.ANY)
    dma = pltpu.SemaphoreType.DMA
    f32 = jnp.float32
    operands = (source, velocity, metric, jnp.asarray(small), jnp.asarray(dft))
    flux, conv = pl.pallas_call(
        functools.partial(kernel, (count, walls, xs_len, chunk, local_len)),
        out_shape=[pltpu.VMEM(out_shape, f32)] * 2,
        in_specs=[anywhere] * 5,
        out_specs=[anywhere] * 2,
        scratch_shapes=[
            pltpu.SMEM(metric.shape, f32),
            pltpu.VMEM(small.shape, f32),
            pltpu.VMEM(velocity.shape, f32),
            pltpu.VMEM((count, 8, local_len), f32),
            pltpu.VMEM((2, xs_len, 8, local_len), f32),
            pltpu.VMEM(blocks, f32),
            pltpu.VMEM((count, 8, local_len), f32),
            pltpu.VMEM((2, count, 8, local_len), f32),
            pltpu.VMEM(dft.shape, jnp.bfloat16),
            pltpu.VMEM((2, 8 * halves, rows, local_len), f32),
            pltpu.VMEM((2, 8 * halves, rows, local_len), f32),
            pltpu.VMEM((6, count, chunk, local_len), f32),
            dma((6,)),
            dma((3, count)),
            dma((3, count)),
            dma((count,)),
            dma((count,)),
            dma((2, xs_len)),
            dma((2, count)),
            dma((6,)),
            dma((6, count)),
            dma((6, count)),
        ],
        compiler_params=pltpu.CompilerParams(
            collective_id=0, has_side_effects=True, vmem_limit_bytes=32 * 2**20
        ),
        name="convect",
    )(*[pltpu.with_memory_space_constraint(x, pltpu.HBM) for x in operands])
    flux, conv = pl.pallas_call(
        store,
        out_shape=[pltpu.HBM(out_shape, f32)] * 2,
        in_specs=[anywhere] * 2,
        out_specs=[anywhere] * 2,
        scratch_shapes=[dma((2,))],
        compiler_params=pltpu.CompilerParams(vmem_limit_bytes=2**20),
        name="store",
    )(flux, conv)
    if chunk % 8:
        planes = [
            out.reshape(xs_len, per_xs, 3, chunk, local_len).transpose(2, 0, 1, 3, 4)
            for out in (flux, conv)
        ]
        flux, conv = [out.reshape(velocity.shape) for out in planes]
    return (conv, flux)


def solution(mesh):
    spec = P(None, None, "wall", "span")
    return jax.shard_map(
        functools.partial(body, mesh.shape["wall"]),
        mesh=mesh,
        in_specs=(spec, P("wall")),
        out_specs=(spec, spec),
        check_vma=False,
    )
```

```python
import functools
import math

import jax
import jax.numpy as jnp
import numpy as np
from jax import lax
from jax.experimental import pallas as pl
from jax.experimental.pallas import tpu as pltpu
from jax.sharding import PartitionSpec as P

MESH = pl.DeviceIdType.MESH


def split_bf16(table):
    high = table.astype(jnp.bfloat16)
    low = (table - np.asarray(high, np.float64)).astype(jnp.bfloat16)
    return high, low


def make_tables(count, local_len):
    total = count * local_len
    halves = count // 2 + 1
    k1 = np.arange(halves, dtype=np.int64)[:, None]
    m = np.arange(local_len, dtype=np.int64)[None, :]
    angle = 2.0 * math.pi / total * (k1 * m % total)
    wave = k1 + count * m
    signed = np.where(wave < total // 2, wave, wave - total)
    weight = np.where((k1 == 0) | (2 * k1 == count), 1.0, 2.0) / total
    keep = (3 * np.abs(signed) < total) * weight
    kappa = 2.0 * math.pi / total * signed * keep
    small = np.stack([np.cos(angle), -np.sin(angle), keep, kappa]).astype(np.float32)
    small = np.pad(small, ((0, 0), (0, -halves % 8), (0, 0)))
    phase = 2.0 * math.pi / local_len * (m.T * m % local_len)
    table = np.concatenate([np.cos(phase), -np.sin(phase)], axis=1)
    return small, np.stack(split_bf16(table))


def weighted(coeffs, values):
    acc = None
    for coeff, value in zip(coeffs, values):
        if abs(coeff) < 1e-12:
            continue
        if abs(abs(coeff) - 1.0) < 1e-12:
            if acc is None:
                acc = value if coeff > 0 else -value
            else:
                acc = acc + value if coeff > 0 else acc - value
        else:
            term = value * np.float32(coeff)
            acc = term if acc is None else acc + term
    return acc


def real_dft(values):
    n = len(values)
    if n == 1:
        return [(values[0], None)]
    half = n // 2
    sums = [values[p] + values[p + half] for p in range(half)]
    diffs = [values[p] - values[p + half] for p in range(half)]
    bins = [None] * (half + 1)
    for index, item in enumerate(real_dft(sums)):
        bins[2 * index] = item
    for k in range(1, half + 1, 2):
        cosines = [math.cos(2 * math.pi * p * k / n) for p in range(half)]
        sines = [-math.sin(2 * math.pi * p * k / n) for p in range(half)]
        bins[k] = (weighted(cosines, diffs), weighted(sines, diffs))
    return bins


def real_inverse(bins, n):
    if n == 1:
        return [bins[0][0]]
    if n == 2:
        return [bins[0][0] + bins[1][0], bins[0][0] - bins[1][0]]
    half = n // 2
    even = real_inverse(bins[0::2], half)
    odd = []
    ks = list(range(1, half, 2))
    for p in range(half):
        coeffs = [math.cos(2 * math.pi * p * k / n) for k in ks]
        coeffs += [-math.sin(2 * math.pi * p * k / n) for k in ks]
        odd.append(weighted(coeffs, [bins[k][0] for k in ks] + [bins[k][1] for k in ks]))
    return [even[p] + odd[p] for p in range(half)] + [even[p] - odd[p] for p in range(half)]


def dft_rows(rows, dft):
    high = rows.astype(jnp.bfloat16)
    low = (rows - high.astype(jnp.float32)).astype(jnp.bfloat16)
    dot = functools.partial(jnp.dot, preferred_element_type=jnp.float32)
    return dot(high, dft[0]) + dot(low, dft[0]) + dot(high, dft[1])


def kernel(
    dims, source, velocity_hbm, metric_hbm, small_hbm, dft_hbm, flux, conv,
    metric, small, planes, ends, wedge, recv, recv_ends, halo, dft, wave_in, wave, obuf,
    local_sem, send_sem, recv_sem, esend_sem, erecv_sem, hsend_sem, hrecv_sem, mine_sem, osend_sem,
    orecv_sem,
):
    count, walls, xs_len, chunk, local_len = dims
    halves = count // 2 + 1
    per_xs = count // xs_len
    span = lax.axis_index("span")
    wall = lax.axis_index("wall")
    place = lax.rem(span, per_xs)
    has_below, has_above = wall > 0, wall < walls - 1

    def wall_at(step):
        return lax.rem(wall + walls + step, walls)

    order = sorted(range(1, count), key=lambda d: abs(d - count // 2))

    def block(ref, index):
        if chunk % 8:
            return ref.at[index]
        at = pl.multiple_of(lax.rem(index, per_xs) * chunk, chunk)
        return ref.at[:, index // per_xs, pl.ds(at, chunk), :]

    barrier = pltpu.get_barrier_semaphore()
    for d in order:
        pl.semaphore_signal(
            barrier, inc=1, device_id=(lax.rem(span + d, count), wall), device_id_type=MESH
        )

    for there, at, step in ((has_below, 0, -1), (has_above, per_xs - 1, 1)):

        @pl.when(there)
        def _():
            @pl.when(place == at)
            def _():
                for p in range(count):
                    pl.semaphore_signal(
                        barrier, inc=1, device_id=(p, wall_at(step)), device_id_type=MESH
                    )

    stage = pltpu.make_async_copy(velocity_hbm, planes, local_sem.at[4])
    stage.start()
    own = pltpu.make_async_copy(block(source, span), recv.at[span], local_sem.at[1])
    own.start()
    load = pltpu.make_async_copy(dft_hbm, dft, local_sem.at[0])
    load.start()
    tables = pltpu.make_async_copy(small_hbm, small, local_sem.at[2])
    tables.start()
    scales = pltpu.make_async_copy(metric_hbm, metric, local_sem.at[3])
    scales.start()

    stage.wait()
    none = jnp.zeros((1, local_len), jnp.float32)

    def plane(x, at):
        if at < 0 or at >= per_xs * chunk:
            return [none] * 3
        return [planes[comp, x, pl.ds(at, 1), :] for comp in range(3)]

    for x in range(xs_len):
        for j in range(per_xs):
            rows = plane(x, j * chunk - 1) + plane(x, (j + 1) * chunk) + [none] * 2
            ends[x * per_xs + j] = jnp.concatenate(rows, axis=0)
        rows = plane(x, per_xs * chunk - 1) + [none] * 5
        wedge[0, x] = jnp.concatenate(rows, axis=0)
        rows = [none] * 3 + plane(x, 0) + [none] * 2
        wedge[1, x] = jnp.concatenate(rows, axis=0)

    sides = (wall + walls - 1) // walls + (2 * walls - 2 - wall) // walls
    pl.semaphore_wait(barrier, count - 1 + xs_len * sides)

    sends = []
    arrivals = [[] for _ in range(3)]
    for comp in range(3):
        for d in order:
            peer = lax.rem(span + d, count)
            copy = pltpu.make_async_remote_copy(
                src_ref=block(source, peer).at[comp],
                dst_ref=recv.at[span, comp],
                send_sem=send_sem.at[comp, d],
                recv_sem=recv_sem.at[comp, d],
                device_id=(peer, wall),
                device_id_type=MESH,
            )
            copy.start()
            arrivals[comp].append(copy)
    for d in order:
        peer = lax.rem(span + d, count)
        copy = pltpu.make_async_remote_copy(
            src_ref=ends.at[peer, pl.ds(0, 6)],
            dst_ref=recv_ends.at[span, pl.ds(0, 6)],
            send_sem=esend_sem.at[d],
            recv_sem=erecv_sem.at[d],
            device_id=(peer, wall),
            device_id_type=MESH,
        )
        copy.start()
        sends.append(copy)
    own_ends = pltpu.make_async_copy(ends.at[span], recv_ends.at[span], local_sem.at[5])
    own_ends.start()

    def halo_copy(side, x):
        if side == 0:
            target = (x * per_xs, wall_at(1))
        else:
            target = (x * per_xs + per_xs - 1, wall_at(-1))
        return pltpu.make_async_remote_copy(
            src_ref=wedge.at[side, x],
            dst_ref=halo.at[side, span],
            send_sem=hsend_sem.at[side, x],
            recv_sem=hrecv_sem.at[side, span],
            device_id=target,
            device_id_type=MESH,
        )

    def halo_arrival(side, p):
        return pltpu.make_async_remote_copy(
            src_ref=wedge.at[side, 0],
            dst_ref=halo.at[side, p],
            send_sem=hsend_sem.at[side, 0],
            recv_sem=hrecv_sem.at[side, p],
            device_id=(p, wall_at(2 * side - 1)),
            device_id_type=MESH,
        )

    for side, there in ((0, has_above), (1, has_below)):

        @pl.when(there)
        def _():
            for x in range(xs_len):
                halo_copy(side, x).start()

    load.wait()
    own.wait()
    tables.wait()
    scales.wait()

    def wait_component(comp):
        for copy in arrivals[comp]:
            copy.wait_recv()

    def wait_edges():
        own_ends.wait()
        for copy in sends:
            copy.wait_recv()
        for side, there, at in ((0, has_below, 0), (1, has_above, per_xs - 1)):

            @pl.when(there)
            def _():
                @pl.when(place == at)
                def _():
                    row = lax.broadcasted_iota(jnp.int32, (8, local_len), 0)
                    taken = row < 3 if side == 0 else row >= 3
                    for p in range(count):
                        halo_arrival(side, p).wait_recv()
                        recv_ends[p] = jnp.where(taken, halo[side, p], recv_ends[p])

    row = lax.broadcasted_iota(jnp.int32, (chunk, local_len), 0)
    scale = jnp.zeros((chunk, local_len), jnp.float32)
    for j in range(chunk):
        scale = jnp.where(row == j, metric[place * chunk + j], scale)

    def velocity(p, comp):
        return recv[p, comp]

    def product(first, second):
        return [velocity(p, first) * velocity(p, second) for p in range(count)]

    def slope(first, second):
        fields = []
        for p in range(count):
            edge = recv_ends[p]
            below = edge[first : first + 1] * edge[second : second + 1]
            above = edge[3 + first : 4 + first] * edge[3 + second : 4 + second]
            inner = velocity(p, first) * velocity(p, second)
            upper = jnp.concatenate([inner[1:], above], axis=0)
            lower = jnp.concatenate([below, inner[:-1]], axis=0)
            fields.append((upper - lower) * scale)
        return fields

    def twiddle(k):
        return small[0, pl.ds(k, 1), :], small[1, pl.ds(k, 1), :]

    def rows_of(ref, start, stop):
        return ref[:, start:stop].reshape(2 * (stop - start) * ref.shape[2], local_len)

    def forward(start, fields):
        for number, values in enumerate(fields):
            for k, (real, imag) in enumerate(real_dft(values)):
                at = (start + number) * halves + k
                tw_cos, tw_sin = twiddle(k)
                if imag is None:
                    wave_in[0, at, 0:chunk, :] = real * tw_cos
                    wave_in[1, at, 0:chunk, :] = real * tw_sin
                else:
                    wave_in[0, at, 0:chunk, :] = real * tw_cos - imag * tw_sin
                    wave_in[1, at, 0:chunk, :] = real * tw_sin + imag * tw_cos
        first, last = start * halves, (start + len(fields)) * halves
        both = dft_rows(rows_of(wave_in, first, last), dft)
        both = both.reshape(2, last - first, wave.shape[2], 2 * local_len)
        by_cos, by_sin = both[..., :local_len], both[..., local_len:]
        wave[0, first:last] = by_cos[0] - by_sin[1]
        wave[1, first:last] = by_sin[0] + by_cos[1]

    copies = []

    def deliver(group, number, filtered):
        slot = 3 * group + number
        for k in range(halves):
            real, imag = filtered(number, k)
            wave_in[0, k] = real
            wave_in[1, k] = imag
        both = dft_rows(rows_of(wave_in, 0, halves), dft)
        both = both.reshape(2, halves, wave.shape[2], 2 * local_len)
        by_cos, by_sin = both[..., :local_len], both[..., local_len:]
        bins = []
        for k in range(halves):
            real = by_cos[0, k] + by_sin[1, k]
            imag = by_cos[1, k] - by_sin[0, k]
            tw_cos, tw_sin = twiddle(k)
            bins.append((real * tw_cos + imag * tw_sin, imag * tw_cos - real * tw_sin))
        for p, value in enumerate(real_inverse(bins, count)):
            obuf[slot, p] = value[0:chunk]
        target = block((flux, conv)[group], span).at[number]
        mine = pltpu.make_async_copy(obuf.at[slot, span], target, mine_sem.at[slot])
        mine.start()
        copies.append(mine)
        for d in order:
            peer = lax.rem(span + d, count)
            copy = pltpu.make_async_remote_copy(
                src_ref=obuf.at[slot, peer],
                dst_ref=target,
                send_sem=osend_sem.at[slot, d],
                recv_sem=orecv_sem.at[slot, d],
                device_id=(peer, wall),
                device_id_type=MESH,
            )
            copy.start()
            copies.append(copy)

    def keep_only(number, k):
        keep = small[2, pl.ds(k, 1), :]
        at = number * halves + k
        return wave[0, at] * keep, wave[1, at] * keep

    def divergence(number, k):
        keep, kappa = small[2, pl.ds(k, 1), :], small[3, pl.ds(k, 1), :]
        at_y = ((3, 4, 6)[number]) * halves + k
        at_z = ((2, 5, 7)[number]) * halves + k
        real = wave[0, at_y] * keep - wave[1, at_z] * kappa
        imag = wave[1, at_y] * keep + wave[0, at_z] * kappa
        return real, imag

    for comp in range(3):
        wait_component(comp)
        forward(comp, [product(0, comp)])
        deliver(0, comp, keep_only)
    wait_edges()
    forward(3, [slope(0, 1)])
    deliver(1, 0, divergence)
    forward(4, [slope(1, 1), product(1, 2)])
    deliver(1, 1, divergence)
    forward(6, [slope(1, 2), product(2, 2)])
    deliver(1, 2, divergence)

    for copy in sum(arrivals, sends):
        copy.wait_send()
    for side, there in ((0, has_above), (1, has_below)):

        @pl.when(there)
        def _():
            for x in range(xs_len):
                halo_copy(side, x).wait_send()

    for copy in copies:
        copy.wait()


def store(flux_in, conv_in, flux, conv, sem):
    copies = [
        pltpu.make_async_copy(flux_in, flux, sem.at[0]),
        pltpu.make_async_copy(conv_in, conv, sem.at[1]),
    ]
    for copy in copies:
        copy.start()
    for copy in copies:
        copy.wait()


def body(walls, velocity, metric):
    count = lax.axis_size("span")
    _, xs_len, yl_len, local_len = velocity.shape
    per_xs = count // xs_len
    chunk = yl_len // per_xs
    halves = count // 2 + 1
    rows = 8 * ((chunk + 7) // 8)
    small, dft = make_tables(count, local_len)

    blocks = (count, 3, chunk, local_len)
    out_shape = velocity.shape
    source = velocity
    if chunk % 8:
        source = velocity.reshape(3, xs_len, per_xs, chunk, local_len)
        source = source.transpose(1, 2, 0, 3, 4).reshape(blocks)
        out_shape = blocks

    anywhere = pl.BlockSpec(memory_space=pl.ANY)
    dma = pltpu.SemaphoreType.DMA
    f32 = jnp.float32
    operands = (source, velocity, metric, jnp.asarray(small), jnp.asarray(dft))
    flux, conv = pl.pallas_call(
        functools.partial(kernel, (count, walls, xs_len, chunk, local_len)),
        out_shape=[pltpu.VMEM(out_shape, f32)] * 2,
        in_specs=[anywhere] * 5,
        out_specs=[anywhere] * 2,
        scratch_shapes=[
            pltpu.SMEM(metric.shape, f32),
            pltpu.VMEM(small.shape, f32),
            pltpu.VMEM(velocity.shape, f32),
            pltpu.VMEM((count, 8, local_len), f32),
            pltpu.VMEM((2, xs_len, 8, local_len), f32),
            pltpu.VMEM(blocks, f32),
            pltpu.VMEM((count, 8, local_len), f32),
            pltpu.VMEM((2, count, 8, local_len), f32),
            pltpu.VMEM(dft.shape, jnp.bfloat16),
            pltpu.VMEM((2, 8 * halves, rows, local_len), f32),
            pltpu.VMEM((2, 8 * halves, rows, local_len), f32),
            pltpu.VMEM((6, count, chunk, local_len), f32),
            dma((6,)),
            dma((3, count)),
            dma((3, count)),
            dma((count,)),
            dma((count,)),
            dma((2, xs_len)),
            dma((2, count)),
            dma((6,)),
            dma((6, count)),
            dma((6, count)),
        ],
        compiler_params=pltpu.CompilerParams(
            collective_id=0, has_side_effects=True, vmem_limit_bytes=32 * 2**20
        ),
        name="convect",
    )(*[pltpu.with_memory_space_constraint(x, pltpu.HBM) for x in operands])
    flux, conv = pl.pallas_call(
        store,
        out_shape=[pltpu.HBM(out_shape, f32)] * 2,
        in_specs=[anywhere] * 2,
        out_specs=[anywhere] * 2,
        scratch_shapes=[dma((2,))],
        compiler_params=pltpu.CompilerParams(vmem_limit_bytes=2**20),
        name="store",
    )(flux, conv)
    if chunk % 8:
        planes = [
            out.reshape(xs_len, per_xs, 3, chunk, local_len).transpose(2, 0, 1, 3, 4)
            for out in (flux, conv)
        ]
        flux, conv = [out.reshape(velocity.shape) for out in planes]
    return (conv, flux)


def solution(mesh):
    spec = P(None, None, "wall", "span")
    return jax.shard_map(
        functools.partial(body, mesh.shape["wall"]),
        mesh=mesh,
        in_specs=(spec, P("wall")),
        out_specs=(spec, spec),
        check_vma=False,
    )
```
